256 devices in a mesh: dp: 8 (over x, core), tm: 32 (over z, y).
Axes of the slice: x: 4, y: 4, z: 8, core: 2. Of those that a mesh axis runs over, the one named last changes fastest.
Arguments:
- latents: bfloat16 [8, 17, 64, 64, 256], P('dp', None, 'tm'), may hold values from -6 to 6
- cotangent: bfloat16 [8, 17, 64, 64, 256], P('dp', None, 'tm'), may hold values from -6 to 6
- spatial_weight: bfloat16 [3, 3, 256, 256], replicated, may hold values from -0.125 to 0.125
- temporal_weight: bfloat16 [3, 256, 256], replicated, may hold values from -0.21875 to 0.21875
Outputs:
- block_out: bfloat16 [8, 17, 64, 64, 256], P('dp', None, 'tm')
- latents_grad: bfloat16 [8, 17, 64, 64, 256], P('dp', None, 'tm')
- spatial_grad: float32 [3, 3, 256, 256], replicated
- temporal_grad: float32 [3, 256, 256], replicated
The draws below stay inside these ranges and needn't reach their ends.
All inputs are finite; a program needn't handle non-finite values.
Results may differ from the reference program's by a relative error of at most 0.0085.
Values may be sent and summed in bfloat16 or wider, within the bound.
A program may use at most 64 MiB of HBM per device.

```python
import jax
import jax.numpy as jnp
from jax import lax

C = 256
FRAMES = 17
W = 64
CLIPS = 8
ROWS = 64


def steps_of(rng, extent, cuts, smallest, high):
    def one(axis_at, blocks):
        heights = jax.random.uniform(jax.random.fold_in(jax.random.fold_in(rng, 6), axis_at), (blocks,), jnp.float32, smallest / len(cuts), high / len(cuts))
        return jnp.repeat(jnp.exp(heights), extent[axis_at] // blocks).reshape((-1,) + (1,) * (len(extent) - axis_at - 1))

    gain = one(*cuts[0])
    for cut in cuts[1:]:
        gain = gain * one(*cut)
    return gain


def normal_values(key, dims, deviation, limit, shards=(), dtype=jnp.bfloat16):
    result = jax.random.normal(key, dims, jnp.float32) * deviation
    if len(shards) > 0:
        result = steps_of(key, dims, shards, -0.22, 0.18) * result
    return jnp.clip(result, min=-limit, max=limit).astype(dtype)


def setup_inputs(seed: int = 0) -> dict:
    key_list = jax.random.split(jax.random.key(seed), 5)
    latents = normal_values(key_list[0], (CLIPS, FRAMES, ROWS, W, C), 1.0, 6.0, ((0, 8), (2, 32)))
    cotangent = normal_values(key_list[1], (CLIPS, FRAMES, ROWS, W, C), 1.0, 6.0, ((0, 8), (2, 32)))
    spatial_weight = normal_values(key_list[2], (3, 3, C, C), (9 * C) ** -0.5, 0.125)
    temporal_weight = normal_values(key_list[3], (3, C, C), (3 * C) ** -0.5, 0.21875)
    return dict(latents=latents, cotangent=cotangent, spatial_weight=spatial_weight, temporal_weight=temporal_weight)


def window_patches(field, flipped):
    padded = jnp.pad(field, ((0, 0), (1, 1), (1, 1), (0, 0)))
    rows = field.shape[1]
    cols = field.shape[2]
    pieces = []
    for first in range(3):
        for second in range(3):
            top = 2 - first if flipped else first
            left = 2 - second if flipped else second
            pieces.append(padded[:, top:top + rows, left:left + cols, :])
    return jnp.concatenate(pieces, axis=3).reshape(-1, 9 * field.shape[3])


def one_clip(inputs):
    latents, cotangent, spatial_weight, temporal_weight = inputs
    frames, rows, cols, chans = latents.shape
    flat_w = spatial_weight.reshape(9 * chans, chans)
    flip_w = jnp.transpose(spatial_weight, (0, 1, 3, 2)).reshape(9 * chans, chans)
    patches = window_patches(latents, False)
    pre = jnp.dot(patches, flat_w, preferred_element_type=jnp.float32)
    act = jax.nn.silu(pre).astype(jnp.bfloat16)
    act3 = act.reshape(frames, rows * cols, chans)
    cot3 = cotangent.reshape(frames, rows * cols, chans)
    act_pad = jnp.pad(act3, ((2, 0), (0, 0), (0, 0)))
    cot_pad = jnp.pad(cot3, ((0, 2), (0, 0), (0, 0)))
    mixed = jnp.zeros((frames * rows * cols, chans), jnp.float32)
    act_grad = jnp.zeros((frames * rows * cols, chans), jnp.float32)
    temporal_parts = []
    cot_flat = cot3.reshape(-1, chans)
    for tap in range(3):
        earlier = act_pad[2 - tap:2 - tap + frames].reshape(-1, chans)
        later = cot_pad[tap:tap + frames].reshape(-1, chans)
        mixed = mixed + jnp.dot(earlier, temporal_weight[tap], preferred_element_type=jnp.float32)
        act_grad = act_grad + jnp.dot(later, temporal_weight[tap].T, preferred_element_type=jnp.float32)
        temporal_parts.append(jnp.dot(earlier.T, cot_flat, preferred_element_type=jnp.float32))
    mixed = mixed.astype(jnp.bfloat16)
    act_grad = act_grad.astype(jnp.bfloat16)
    block_out = (latents.reshape(-1, chans).astype(jnp.float32) + mixed.astype(jnp.float32)).astype(jnp.bfloat16)
    sig = jax.nn.sigmoid(pre)
    pre_grad = (act_grad.astype(jnp.float32) * sig * (1.0 + pre * (1.0 - sig))).astype(jnp.bfloat16)
    back = jnp.dot(window_patches(pre_grad.reshape(frames, rows, cols, chans), True), flip_w, preferred_element_type=jnp.float32)
    latents_grad = (cotangent.reshape(-1, chans).astype(jnp.float32) + back).astype(jnp.bfloat16)
    spatial_part = jnp.dot(patches.T, pre_grad, preferred_element_type=jnp.float32)
    return (block_out.reshape(latents.shape), latents_grad.reshape(latents.shape), spatial_part, jnp.stack(temporal_parts))


def reference(latents, cotangent, spatial_weight, temporal_weight):
    clips, frames, rows, cols, chans = latents.shape
    weights_s = jnp.broadcast_to(spatial_weight, (clips,) + spatial_weight.shape)
    weights_t = jnp.broadcast_to(temporal_weight, (clips,) + temporal_weight.shape)
    block_out, latents_grad, spatial_parts, temporal_parts = lax.map(one_clip, (latents, cotangent, weights_s, weights_t))
    scale = (clips * frames * rows * cols) ** -0.5
    spatial_grad = jnp.sum(spatial_parts, axis=0) * scale
    temporal_grad = jnp.sum(temporal_parts, axis=0) * scale
    return (block_out, latents_grad, spatial_grad.reshape(3, 3, chans, chans), temporal_grad)
```

```python
import jax
import jax.numpy as jnp
from jax import lax
from jax.experimental import pallas as pl
from jax.experimental.pallas import tpu as pltpu
from jax.sharding import PartitionSpec as P

F32 = jnp.float32
BF16 = jnp.bfloat16
NX, NY, NZ = 4, 4, 8
FRAMES, COLS, CH = 17, 64, 256
PAIRS = FRAMES // 2

CORE, XF, XB, XF2, ZS, YS, ZG, XG, CG, SLOTS = 0, 1, 2, 3, 4, 11, 14, 21, 24, 25


def peer(dp, tm):
    return (dp, tm)


def remote(src, dst, send, recv, device):
    return pltpu.make_async_remote_copy(
        src_ref=src, dst_ref=dst, send_sem=send, recv_sem=recv,
        device_id=device, device_id_type=pl.DeviceIdType.MESH,
    )


class Reduce:
    def __init__(self, here, grads, total, c_send, c_recv, x_send, x_recv, z_send, z_recv, y_buf, ssem, rsem):
        self.x, self.core, self.z, self.y = here
        self.grads, self.total = grads, total
        self.c_send, self.c_recv = c_send, c_recv
        self.x_send, self.x_recv = x_send, x_recv
        self.z_send, self.z_recv, self.y_buf = z_send, z_recv, y_buf
        self.ssem, self.rsem = ssem, rsem
        self.step = 1 - 2 * self.core
        self.copies = {}
        self.fwd = lax.rem(self.x + self.step + NX, NX)
        self.bwd = lax.rem(self.x - self.step + NX, NX)
        self.far = lax.rem(self.x + 2, NX)
        self.tm = self.z * NY + self.y

    def at_x(self, x):
        return peer(x * 2 + self.core, self.tm)

    def at_z(self, j):
        z = lax.rem(self.z + j, NZ)
        return z, peer(self.x * 2 + self.core, z * NY + self.y)

    def at_y(self, j):
        return peer(self.x * 2 + self.core, self.z * NY + lax.rem(self.y + j, NY))

    def partner(self):
        return peer(self.x * 2 + 1 - self.core, self.tm)

    def send(self, s, slot, src, dst, device):
        copy = remote(src, dst, self.ssem.at[s, slot], self.rsem.at[s, slot], device)
        copy.start()
        self.copies[s, slot] = copy

    def arrive(self, s, *slots):
        for slot in slots:
            self.copies[s, slot].wait_recv()

    def finish(self):
        for copy in self.copies.values():
            copy.wait_send()

    def tile(self, s):
        return self.core * 3 + s

    def stages(self, s):
        return self.x_first(s) if s < 2 else self.z_first(s)

    def core_out(self, s):
        other = (1 - self.core) * 3 + s
        self.c_send[s] = self.grads[other].astype(BF16)
        self.send(s, CORE, self.c_send.at[s], self.c_recv.at[s], self.partner())

    def core_back(self, s):
        t = self.tile(s)
        self.send(s, CG, self.total.at[t], self.total.at[t], self.partner())

    def y_out(self, s, value):
        self.y_buf[s, self.y] = value.astype(BF16)
        for j in range(1, NY):
            self.send(s, YS + j - 1, self.y_buf.at[s, self.y], self.y_buf.at[s, self.y], self.at_y(j))

    def y_sum(self, s):
        self.arrive(s, *range(YS, YS + NY - 1))
        value = self.y_buf[s, 0].astype(F32)
        for j in range(1, NY):
            value = value + self.y_buf[s, j].astype(F32)
        return value.astype(BF16)

    def x_first(self, s):
        t = self.tile(s)

        def local(x):
            return self.grads[t, x] + self.c_recv[s, x].astype(F32)

        def first():
            self.arrive(s, CORE)
            self.x_send[s, 0] = local(self.far).astype(BF16)
            self.send(s, XF, self.x_send.at[s, 0], self.x_recv.at[s, 0], self.at_x(self.fwd))
            self.x_send[s, 1] = local(self.bwd).astype(BF16)
            self.send(s, XB, self.x_send.at[s, 1], self.x_recv.at[s, 1], self.at_x(self.bwd))

        def second():
            self.arrive(s, XF)
            self.x_send[s, 2] = (local(self.fwd) + self.x_recv[s, 0].astype(F32)).astype(BF16)
            self.send(s, XF2, self.x_send.at[s, 2], self.x_recv.at[s, 2], self.at_x(self.fwd))

        def third():
            self.arrive(s, XB, XF2)
            own = local(self.x) + self.x_recv[s, 1].astype(F32) + self.x_recv[s, 2].astype(F32)
            self.grads[t, self.x] = own
            self.z_send[s, 0] = own.astype(BF16)
            for j in (4, 3, 5, 2, 6, 1, 7):
                z, device = self.at_z(j)
                self.send(s, ZS + j - 1, self.z_send.at[s, 0, z], self.z_recv.at[s, j - 1, 0], device)

        def fourth():
            self.arrive(s, *range(ZS, ZS + NZ - 1))
            own = self.grads[t, self.x, self.z]
            for j in range(NZ - 1):
                own = own + self.z_recv[s, j, 0].astype(F32)
            self.y_out(s, own)

        def fifth():
            self.total[t, self.x, self.z] = self.y_sum(s)
            block = self.total.at[t, self.x, self.z]
            for j in (4, 3, 5, 2, 6, 1, 7):
                self.send(s, ZG + j - 1, block, block, self.at_z(j)[1])

        def sixth():
            self.arrive(s, *range(ZG, ZG + NZ - 1))
            self.x_spread(s, lambda x: self.total.at[t, x])

        def seventh():
            self.x_forward(s, lambda x: self.total.at[t, x])

        def eighth():
            self.arrive(s, XG + 1, XG + 2)
            self.core_back(s)

        return [lambda: self.core_out(s), first, second, third, fourth, fifth, sixth, seventh, eighth, lambda: self.arrive(s, CG)]

    def x_spread(self, s, block):
        mine = block(self.x)
        self.send(s, XG, mine, mine, self.at_x(self.fwd))
        self.send(s, XG + 1, mine, mine, self.at_x(self.bwd))

    def x_forward(self, s, block):
        self.arrive(s, XG)
        got = block(self.bwd)
        self.send(s, XG + 2, got, got, self.at_x(self.fwd))

    def z_first(self, s):
        t = self.tile(s)

        def chunk(z):
            return z // 2, pl.ds(lax.rem(z, 2) * NX, NX)

        def cell(x):
            return self.z // 2, lax.rem(self.z, 2) * NX + x

        def first():
            self.arrive(s, CORE)
            self.z_send[s] = (self.grads[t] + self.c_recv[s].astype(F32)).astype(BF16)
            for j in (4, 3, 5, 2, 6, 1, 7):
                z, device = self.at_z(j)
                self.send(s, ZS + j - 1, self.z_send.at[(s, *chunk(z))], self.z_recv.at[s, j - 1], device)

        def second():
            self.arrive(s, *range(ZS, ZS + NZ - 1))
            where = chunk(self.z)
            own = self.grads[(t, *where)] + self.c_recv[(s, *where)].astype(F32)
            for j in range(NZ - 1):
                own = own + self.z_recv[s, j].astype(F32)
            self.grads[(t, *where)] = own
            self.x_send[s, 0, 0] = self.grads[(t, *cell(self.far))].astype(BF16)
            self.send(s, XF, self.x_send.at[s, 0, 0], self.x_recv.at[s, 0, 0], self.at_x(self.fwd))
            self.x_send[s, 1, 0] = self.grads[(t, *cell(self.bwd))].astype(BF16)
            self.send(s, XB, self.x_send.at[s, 1, 0], self.x_recv.at[s, 1, 0], self.at_x(self.bwd))

        def third():
            self.arrive(s, XF)
            self.x_send[s, 2, 0] = (self.grads[(t, *cell(self.fwd))] + self.x_recv[s, 0, 0].astype(F32)).astype(BF16)
            self.send(s, XF2, self.x_send.at[s, 2, 0], self.x_recv.at[s, 2, 0], self.at_x(self.fwd))

        def fourth():
            self.arrive(s, XB, XF2)
            own = self.grads[(t, *cell(self.x))] + self.x_recv[s, 1, 0].astype(F32) + self.x_recv[s, 2, 0].astype(F32)
            self.y_out(s, own)

        def fifth():
            self.total[(t, *cell(self.x))] = self.y_sum(s)
            self.x_spread(s, lambda x: self.total.at[(t, *cell(x))])

        def sixth():
            self.x_forward(s, lambda x: self.total.at[(t, *cell(x))])

        def seventh():
            self.arrive(s, XG + 1, XG + 2)
            block = self.total.at[(t, *chunk(self.z))]
            for j in (4, 3, 5, 2, 6, 1, 7):
                self.send(s, ZG + j - 1, block, block, self.at_z(j)[1])

        def eighth():
            self.arrive(s, *range(ZG, ZG + NZ - 1))
            self.core_back(s)

        return [lambda: self.core_out(s), first, second, third, fourth, fifth, sixth, seventh, eighth, lambda: self.arrive(s, CG)]


REDUCE_SCRATCH = [
    pltpu.VMEM((6, 4, 8, 32, 128), F32),
    pltpu.VMEM((6, 4, 8, 32, 128), BF16),
    pltpu.VMEM((3, 4, 8, 32, 128), BF16),
    pltpu.VMEM((3, 4, 8, 32, 128), BF16),
    pltpu.VMEM((3, 3, 8, 32, 128), BF16),
    pltpu.VMEM((3, 3, 8, 32, 128), BF16),
    pltpu.VMEM((3, 4, 8, 32, 128), BF16),
    pltpu.VMEM((3, 7, 4, 32, 128), BF16),
    pltpu.VMEM((3, 4, 32, 128), BF16),
    pltpu.SemaphoreType.DMA((3, SLOTS)),
    pltpu.SemaphoreType.DMA((3, SLOTS)),
]


def position():
    dp, tm = lax.axis_index("dp"), lax.axis_index("tm")
    return dp // 2, lax.rem(dp, 2), tm // NY, lax.rem(tm, NY)


def greet(x, core, z, y, extra=()):
    barrier = pltpu.get_barrier_semaphore()
    tm = z * NY + y
    peers = [peer(x * 2 + 1 - core, tm)]
    peers += [peer(lax.rem(x + j, NX) * 2 + core, tm) for j in (1, NX - 1)]
    peers += [peer(x * 2 + core, z * NY + lax.rem(y + j, NY)) for j in range(1, NY)]
    peers += [peer(x * 2 + core, lax.rem(z + j, NZ) * NY + y) for j in range(1, NZ)]
    peers += list(extra)
    for device in peers:
        pl.semaphore_signal(barrier, inc=1, device_id=device, device_id_type=pl.DeviceIdType.MESH)
    return barrier, len(peers)


NT = (((1,), (1,)), ((), ()))
TN = (((0,), (0,)), ((), ()))


def dot(a, b, dims=(((1,), (0,)), ((), ()))):
    return lax.dot_general(a, b, dims, preferred_element_type=F32)


def shifted(value, up):
    cells = value.shape[0]
    col = lax.rem(lax.broadcasted_iota(jnp.int32, value.shape, 0), COLS)
    if up:
        return jnp.where(col == 0, 0.0, pltpu.roll(value, 1, 0))
    return jnp.where(col == COLS - 1, 0.0, pltpu.roll(value, cells - 1, 0))


def kernel(
    lat, cot, weight, mix, block_out, lat_grad, grad_out,
    ext, cotx, actx, agrad, pg3, pgh, w_v, mix_v, out_b, out_g,
    grads, total, c_send, c_recv, x_send, x_recv, z_send, z_recv, y_buf, ssem, rsem,
    load_sem, halo_s, halo_r, back_s, back_r, store_sem,
):
    here = position()
    x, core, z, y = here
    dp, tm = x * 2 + core, z * NY + y
    bands = NZ * NY
    below = peer(dp, lax.rem(tm + 1, bands))
    above = peer(dp, lax.rem(tm + bands - 1, bands))
    barrier, count = greet(x, core, z, y, (above, below))

    loads = [
        pltpu.make_async_copy(cot, cotx.at[pl.ds(0, FRAMES)], load_sem.at[0]),
        pltpu.make_async_copy(mix, mix_v, load_sem.at[1]),
        pltpu.make_async_copy(lat, ext.at[:, pl.ds(1, 2)], load_sem.at[2]),
    ]
    for a in range(3):
        for b in range(3):
            loads.append(pltpu.make_async_copy(weight.at[a, b], w_v.at[a, :, pl.ds(b * CH, CH)], load_sem.at[3 + a * 3 + b]))
    for load in loads:
        load.start()
    cotx[FRAMES:] = jnp.zeros((2, 2 * COLS, CH), BF16)
    actx[:2] = jnp.zeros((2, 2 * COLS, CH), BF16)
    pl.semaphore_wait(barrier, count)

    def halo(i, first, size):
        frames = pl.ds(first, size)
        return (
            remote(lat.at[frames, 1], ext.at[frames, 0], halo_s.at[0, i], halo_r.at[0, i], below),
            remote(lat.at[frames, 0], ext.at[frames, 3], halo_s.at[1, i], halo_r.at[1, i], above),
        )

    def grad_halo(i, first, size):
        frames = pl.ds(first, size)
        return (
            remote(pg3.at[frames, 2, :, pl.ds(CH, CH)], pgh.at[0, frames], back_s.at[0, i], back_r.at[0, i], below),
            remote(pg3.at[frames, 1, :, pl.ds(CH, CH)], pgh.at[1, frames], back_s.at[1, i], back_r.at[1, i], above),
        )

    def over(make, act):
        @pl.loop(0, PAIRS)
        def _(i):
            for copy in make(i, 2 * i, 2):
                act(copy)
        for copy in make(PAIRS, FRAMES - 1, 1):
            act(copy)

    over(halo, lambda copy: copy.start())

    loads[0].wait()
    loads[1].wait()

    @pl.loop(0, 3)
    def _(i):
        first = jnp.minimum(6 * i, FRAMES - 6)
        value = jnp.zeros((6 * 2 * COLS, CH), F32)
        for k in range(3):
            value = value + dot(cotx[pl.ds(first + k, 6)].reshape(-1, CH), mix_v[k], NT)
        agrad[pl.ds(first, 6)] = value.astype(BF16).reshape(6, 2 * COLS, CH)

    for load in loads[2:]:
        load.wait()

    grads[...] = jnp.zeros_like(grads)

    def add_grad(index, value):
        for t in range(6):
            grads[t, index] += value[:, t * 128 : (t + 1) * 128].reshape(8, 32, 128)

    def chunk(i, first, size):
        for copy in halo(i, first, size):
            copy.wait_recv()
        frames = pl.ds(first, size)
        cells = size * 2 * COLS

        @pl.when(tm == 0)
        def _():
            ext[frames, 0] = jnp.zeros((size, COLS, CH), BF16)

        @pl.when(tm == bands - 1)
        def _():
            ext[frames, 3] = jnp.zeros((size, COLS, CH), BF16)

        parts = jnp.zeros((cells, 3 * CH), F32)
        for a in range(3):
            parts = parts + dot(ext[frames, a : a + 2].reshape(cells, CH), w_v[a])
        pre = shifted(parts[:, :CH], True) + parts[:, CH : 2 * CH] + shifted(parts[:, 2 * CH :], False)
        sig = jax.nn.sigmoid(pre)
        act = (pre * sig).astype(BF16)
        actx[pl.ds(first + 2, size)] = act.reshape(size, 2 * COLS, CH)
        ag = agrad[frames].reshape(cells, CH).astype(F32)
        pg = ag * sig * (1.0 + pre * (1.0 - sig))
        three = jnp.concatenate([shifted(pg, False), pg, shifted(pg, True)], axis=1).astype(BF16)
        pg3[frames, 1:3] = three.reshape(size, 2, COLS, 3 * CH)
        for a in range(3):
            add_grad(a, dot(ext[frames, a : a + 2].reshape(cells, CH), three, TN))
        cots = jnp.concatenate([cotx[pl.ds(first + k, size)].reshape(cells, CH) for k in range(3)], axis=1)
        add_grad(3, dot(act, cots, TN))

    @pl.loop(0, PAIRS)
    def _(i):
        chunk(i, 2 * i, 2)

    chunk(PAIRS, FRAMES - 1, 1)
    over(grad_halo, lambda copy: copy.start())

    def mix_unit(i, first, size):
        frames = pl.ds(first, size)
        value = jnp.zeros((size * 2 * COLS, CH), F32)
        for k in range(3):
            value = value + dot(actx[pl.ds(first + 2 - k, size)].reshape(-1, CH), mix_v[k])
        value = value.astype(BF16).astype(F32) + ext[frames, 1:3].reshape(-1, CH).astype(F32)
        out_b[frames] = value.astype(BF16).reshape(size, 2 * COLS, CH)
        pltpu.make_async_copy(out_b.at[frames], block_out.at[frames], store_sem.at[0, i]).start()

    def back_unit(i, first, size):
        frames = pl.ds(first, size)
        cells = size * 2 * COLS
        for copy in grad_halo(i, first, size):
            copy.wait_recv()
        for side, row, edge in ((0, 0, 0), (1, 3, bands - 1)):
            value = pgh[side, frames].reshape(size * COLS, CH).astype(F32)
            value = jnp.where(tm == edge, 0.0, value)
            three = jnp.concatenate([shifted(value, False), value, shifted(value, True)], axis=1)
            pg3[frames, row] = three.astype(BF16).reshape(size, COLS, 3 * CH)
        value = cotx[frames].reshape(cells, CH).astype(F32)
        back = jnp.zeros((cells, CH), F32)
        for a in range(3):
            back = back + dot(pg3[frames, 2 - a : 4 - a].reshape(cells, 3 * CH), w_v[a], NT)
        out_g[frames] = (value + back).astype(BF16).reshape(size, 2 * COLS, CH)
        pltpu.make_async_copy(out_g.at[frames], lat_grad.at[frames], store_sem.at[1, i]).start()

    def units(unit, low, high):
        if low < min(high, PAIRS):
            @pl.loop(low, min(high, PAIRS))
            def _(i):
                unit(i, 2 * i, 2)
        if high > PAIRS:
            unit(PAIRS, FRAMES - 1, 1)

    reduce = Reduce(here, grads, total, c_send, c_recv, x_send, x_recv, z_send, z_recv, y_buf, ssem, rsem)
    steps = [reduce.stages(s) for s in range(3)]
    filler = {0: (mix_unit, 0, 3), 1: (mix_unit, 3, 9), 2: (back_unit, 0, 2), 3: (back_unit, 2, 5), 4: (back_unit, 5, 7), 5: (back_unit, 7, 9)}
    for stage in range(10):
        for s in (2, 0, 1):
            steps[s][stage]()
        if stage in filler:
            units(*filler[stage])

    outs = []
    for t in range(6):
        b, half = t // 2, t % 2
        out = pltpu.make_async_copy(total.at[t], grad_out.at[:, b, :, :, pl.ds(half * 128, 128)], load_sem.at[t])
        out.start()
        outs.append(out)
    reduce.finish()
    over(halo, lambda copy: copy.wait_send())
    over(grad_halo, lambda copy: copy.wait_send())

    def stores(i, first, size):
        frames = pl.ds(first, size)
        return (
            pltpu.make_async_copy(out_b.at[frames], block_out.at[frames], store_sem.at[0, i]),
            pltpu.make_async_copy(out_g.at[frames], lat_grad.at[frames], store_sem.at[1, i]),
        )

    over(stores, lambda copy: copy.wait())
    for out in outs:
        out.wait()


def body(latents, cotangent, spatial_weight, temporal_weight):
    clips, frames, rows, cols, chans = latents.shape
    cells = rows * cols
    any_spec = pl.BlockSpec(memory_space=pl.ANY)
    half = jax.ShapeDtypeStruct((frames, cells, chans), BF16)
    block_out, lat_grad, grad = pl.pallas_call(
        kernel,
        out_shape=(half, half, jax.ShapeDtypeStruct((4, 3, 8, 32, 256), BF16)),
        in_specs=[any_spec] * 4,
        out_specs=(any_spec,) * 3,
        scratch_shapes=[
            pltpu.VMEM((frames, 4, cols, chans), BF16),
            pltpu.VMEM((frames + 2, cells, chans), BF16),
            pltpu.VMEM((frames + 2, cells, chans), BF16),
            pltpu.VMEM((frames, cells, chans), BF16),
            pltpu.VMEM((frames, 4, cols, 3 * chans), BF16),
            pltpu.VMEM((2, frames, cols, chans), BF16),
            pltpu.VMEM((3, chans, 3 * chans), BF16),
            pltpu.VMEM((3, chans, chans), BF16),
            pltpu.VMEM((frames, cells, chans), BF16),
            pltpu.VMEM((frames, cells, chans), BF16),
            *REDUCE_SCRATCH,
            pltpu.SemaphoreType.DMA((12,)),
            pltpu.SemaphoreType.DMA((2, PAIRS + 1)),
            pltpu.SemaphoreType.DMA((2, PAIRS + 1)),
            pltpu.SemaphoreType.DMA((2, PAIRS + 1)),
            pltpu.SemaphoreType.DMA((2, PAIRS + 1)),
            pltpu.SemaphoreType.DMA((2, PAIRS + 1)),
        ],
        compiler_params=pltpu.CompilerParams(
            collective_id=0, has_side_effects=True, vmem_limit_bytes=60 * 1024 * 1024
        ),
    )(
        latents.reshape(frames, rows, cols, chans),
        cotangent.reshape(frames, cells, chans),
        spatial_weight,
        temporal_weight,
    )
    scale = (clips * lax.axis_size("dp") * frames * rows * lax.axis_size("tm") * cols) ** (-0.5)
    grad = grad.reshape(4, 3, chans, chans)
    return (
        block_out.reshape(latents.shape),
        lat_grad.reshape(latents.shape),
        grad[:3].astype(F32) * scale,
        grad[3].astype(F32) * scale,
    )


def solution(mesh):
    in_specs = (P("dp", None, "tm", None, None), P("dp", None, "tm", None, None), P(), P())
    return jax.shard_map(body, mesh=mesh, in_specs=in_specs, out_specs=in_specs, check_vma=False)
```

```python
import functools

import jax
import jax.numpy as jnp
from jax import lax
from jax.experimental import pallas as pl
from jax.experimental.pallas import tpu as pltpu
from jax.sharding import PartitionSpec as P

F32 = jnp.float32
BF16 = jnp.bfloat16
NX, NY, NZ = 4, 4, 8
FRAMES, COLS, CH = 17, 64, 256
VMEM_LIMIT = 56 * 1024 * 1024
PAIRS = FRAMES // 2

CORE, XF, XB, XF2, ZS, YS, ZG, XG, CG, SLOTS = 0, 1, 2, 3, 4, 11, 14, 21, 24, 25


def peer(dp, tm):
    return (dp, tm)


def remote(src, dst, send, recv, device):
    return pltpu.make_async_remote_copy(
        src_ref=src, dst_ref=dst, send_sem=send, recv_sem=recv,
        device_id=device, device_id_type=pl.DeviceIdType.MESH,
    )


class Reduce:
    def __init__(self, here, grads, total, c_send, c_recv, x_send, x_recv, z_send, z_recv, y_buf, ssem, rsem):
        self.x, self.core, self.z, self.y = here
        self.grads, self.total = grads, total
        self.c_send, self.c_recv = c_send, c_recv
        self.x_send, self.x_recv = x_send, x_recv
        self.z_send, self.z_recv, self.y_buf = z_send, z_recv, y_buf
        self.ssem, self.rsem = ssem, rsem
        self.step = 1 - 2 * self.core
        self.copies = {}
        self.fwd = lax.rem(self.x + self.step + NX, NX)
        self.bwd = lax.rem(self.x - self.step + NX, NX)
        self.far = lax.rem(self.x + 2, NX)
        self.tm = self.z * NY + self.y

    def at_x(self, x):
        return peer(x * 2 + self.core, self.tm)

    def at_z(self, j):
        z = lax.rem(self.z + j, NZ)
        return z, peer(self.x * 2 + self.core, z * NY + self.y)

    def at_y(self, j):
        return peer(self.x * 2 + self.core, self.z * NY + lax.rem(self.y + j, NY))

    def partner(self):
        return peer(self.x * 2 + 1 - self.core, self.tm)

    def send(self, s, slot, src, dst, device):
        copy = remote(src, dst, self.ssem.at[s, slot], self.rsem.at[s, slot], device)
        copy.start()
        self.copies[s, slot] = copy

    def arrive(self, s, *slots):
        for slot in slots:
            self.copies[s, slot].wait_recv()

    def finish(self):
        for copy in self.copies.values():
            copy.wait_send()

    def tile(self, s):
        return self.core * 3 + s

    def stages(self, s):
        return self.x_first(s)

    def core_out(self, s):
        other = (1 - self.core) * 3 + s
        self.c_send[s] = self.grads[other].astype(BF16)
        self.send(s, CORE, self.c_send.at[s], self.c_recv.at[s], self.partner())

    def core_back(self, s):
        t = self.tile(s)
        self.send(s, CG, self.total.at[t], self.total.at[t], self.partner())

    def y_out(self, s, value):
        self.y_buf[s, self.y] = value.astype(BF16)
        for j in range(1, NY):
            self.send(s, YS + j - 1, self.y_buf.at[s, self.y], self.y_buf.at[s, self.y], self.at_y(j))

    def y_sum(self, s):
        self.arrive(s, *range(YS, YS + NY - 1))
        value = self.y_buf[s, 0].astype(F32)
        for j in range(1, NY):
            value = value + self.y_buf[s, j].astype(F32)
        return value.astype(BF16)

    def x_first(self, s):
        t = self.tile(s)

        def local(x):
            return self.grads[t, x] + self.c_recv[s, x].astype(F32)

        def first():
            self.arrive(s, CORE)
            self.x_send[s, 0] = local(self.far).astype(BF16)
            self.send(s, XF, self.x_send.at[s, 0], self.x_recv.at[s, 0], self.at_x(self.fwd))
            self.x_send[s, 1] = local(self.bwd).astype(BF16)
            self.send(s, XB, self.x_send.at[s, 1], self.x_recv.at[s, 1], self.at_x(self.bwd))

        def second():
            self.arrive(s, XF)
            self.x_send[s, 2] = (local(self.fwd) + self.x_recv[s, 0].astype(F32)).astype(BF16)
            self.send(s, XF2, self.x_send.at[s, 2], self.x_recv.at[s, 2], self.at_x(self.fwd))

        def third():
            self.arrive(s, XB, XF2)
            own = local(self.x) + self.x_recv[s, 1].astype(F32) + self.x_recv[s, 2].astype(F32)
            self.grads[t, self.x] = own
            self.z_send[s, 0] = own.astype(BF16)
            for j in (4, 3, 5, 2, 6, 1, 7):
                z, device = self.at_z(j)
                self.send(s, ZS + j - 1, self.z_send.at[s, 0, z], self.z_recv.at[s, j - 1, 0], device)

        def fourth():
            self.arrive(s, *range(ZS, ZS + NZ - 1))
            own = self.grads[t, self.x, self.z]
            for j in range(NZ - 1):
                own = own + self.z_recv[s, j, 0].astype(F32)
            self.y_out(s, own)

        def fifth():
            self.total[t, self.x, self.z] = self.y_sum(s)
            block = self.total.at[t, self.x, self.z]
            for j in (4, 3, 5, 2, 6, 1, 7):
                self.send(s, ZG + j - 1, block, block, self.at_z(j)[1])

        def sixth():
            self.arrive(s, *range(ZG, ZG + NZ - 1))
            self.x_spread(s, lambda x: self.total.at[t, x])

        def seventh():
            self.x_forward(s, lambda x: self.total.at[t, x])

        def eighth():
            self.arrive(s, XG + 1, XG + 2)
            self.core_back(s)

        return [lambda: self.core_out(s), first, second, third, fourth, fifth, sixth, seventh, eighth, lambda: self.arrive(s, CG)]

    def x_spread(self, s, block):
        mine = block(self.x)
        self.send(s, XG, mine, mine, self.at_x(self.fwd))
        self.send(s, XG + 1, mine, mine, self.at_x(self.bwd))

    def x_forward(self, s, block):
        self.arrive(s, XG)
        got = block(self.bwd)
        self.send(s, XG + 2, got, got, self.at_x(self.fwd))


REDUCE_SCRATCH = [
    pltpu.VMEM((6, 4, 8, 32, 128), F32),
    pltpu.VMEM((3, 4, 8, 32, 128), BF16),
    pltpu.VMEM((3, 4, 8, 32, 128), BF16),
    pltpu.VMEM((3, 3, 8, 32, 128), BF16),
    pltpu.VMEM((3, 3, 8, 32, 128), BF16),
    pltpu.VMEM((3, 4, 8, 32, 128), BF16),
    pltpu.VMEM((3, 7, 4, 32, 128), BF16),
    pltpu.VMEM((3, 4, 32, 128), BF16),
    pltpu.SemaphoreType.DMA((3, SLOTS)),
    pltpu.SemaphoreType.DMA((3, SLOTS)),
]


def position():
    dp, tm = lax.axis_index("dp"), lax.axis_index("tm")
    return dp // 2, lax.rem(dp, 2), tm // NY, lax.rem(tm, NY)


def greet(x, core, z, y, extra=()):
    barrier = pltpu.get_barrier_semaphore()
    tm = z * NY + y
    peers = [peer(x * 2 + 1 - core, tm)]
    peers += [peer(lax.rem(x + j, NX) * 2 + core, tm) for j in (1, NX - 1)]
    peers += [peer(x * 2 + core, z * NY + lax.rem(y + j, NY)) for j in range(1, NY)]
    peers += [peer(x * 2 + core, lax.rem(z + j, NZ) * NY + y) for j in range(1, NZ)]
    peers += list(extra)
    for device in peers:
        pl.semaphore_signal(barrier, inc=1, device_id=device, device_id_type=pl.DeviceIdType.MESH)
    return barrier, len(peers)


NT = (((1,), (1,)), ((), ()))
TN = (((0,), (0,)), ((), ()))


def dot(a, b, dims=(((1,), (0,)), ((), ()))):
    return lax.dot_general(a, b, dims, preferred_element_type=F32)


def shifted(value, up):
    cells = value.shape[0]
    col = lax.rem(lax.broadcasted_iota(jnp.int32, value.shape, 0), COLS)
    if up:
        return jnp.where(col == 0, 0.0, pltpu.roll(value, 1, 0))
    return jnp.where(col == COLS - 1, 0.0, pltpu.roll(value, cells - 1, 0))


def kernel(
    lat, cot, weight, mix, out_b, out_g, total,
    ext, cotx, actx, agrad, pg3, pgh, w_v, mix_v,
    grads, c_send, c_recv, x_send, x_recv, z_send, z_recv, y_buf, ssem, rsem,
    load_sem, halo_s, halo_r, back_s, back_r,
):
    here = position()
    x, core, z, y = here
    dp, tm = x * 2 + core, z * NY + y
    bands = NZ * NY
    below = peer(dp, lax.rem(tm + 1, bands))
    above = peer(dp, lax.rem(tm + bands - 1, bands))
    barrier, count = greet(x, core, z, y, (above, below))

    loads = [
        pltpu.make_async_copy(cot, cotx.at[pl.ds(0, FRAMES)], load_sem.at[0]),
        pltpu.make_async_copy(mix, mix_v, load_sem.at[1]),
        pltpu.make_async_copy(lat, ext.at[:, pl.ds(1, 2)], load_sem.at[2]),
    ]
    for a in range(3):
        for b in range(3):
            loads.append(pltpu.make_async_copy(weight.at[a, b], w_v.at[a, :, pl.ds(b * CH, CH)], load_sem.at[3 + a * 3 + b]))
    for load in loads:
        load.start()
    cotx[FRAMES:] = jnp.zeros((2, 2 * COLS, CH), BF16)
    actx[:2] = jnp.zeros((2, 2 * COLS, CH), BF16)
    pl.semaphore_wait(barrier, count)

    def halo(i, first, size):
        frames = pl.ds(first, size)
        return (
            remote(lat.at[frames, 1], ext.at[frames, 0], halo_s.at[0, i], halo_r.at[0, i], below),
            remote(lat.at[frames, 0], ext.at[frames, 3], halo_s.at[1, i], halo_r.at[1, i], above),
        )

    def grad_halo(i, first, size):
        frames = pl.ds(first, size)
        return (
            remote(pg3.at[frames, 2, :, pl.ds(CH, CH)], pgh.at[0, frames], back_s.at[0, i], back_r.at[0, i], below),
            remote(pg3.at[frames, 1, :, pl.ds(CH, CH)], pgh.at[1, frames], back_s.at[1, i], back_r.at[1, i], above),
        )

    def over(make, act):
        @pl.loop(0, PAIRS)
        def _(i):
            for copy in make(i, 2 * i, 2):
                act(copy)
        for copy in make(PAIRS, FRAMES - 1, 1):
            act(copy)

    over(halo, lambda copy: copy.start())

    loads[0].wait()
    loads[1].wait()

    @pl.loop(0, 3)
    def _(i):
        first = jnp.minimum(6 * i, FRAMES - 6)
        value = jnp.zeros((6 * 2 * COLS, CH), F32)
        for k in range(3):
            value = value + dot(cotx[pl.ds(first + k, 6)].reshape(-1, CH), mix_v[k], NT)
        agrad[pl.ds(first, 6)] = value.astype(BF16).reshape(6, 2 * COLS, CH)

    for load in loads[2:]:
        load.wait()

    grads[...] = jnp.zeros_like(grads)

    def add_grad(index, value):
        for t in range(6):
            grads[t, index] += value[:, t * 128 : (t + 1) * 128].reshape(8, 32, 128)

    def chunk(i, first, size):
        for copy in halo(i, first, size):
            copy.wait_recv()
        frames = pl.ds(first, size)
        cells = size * 2 * COLS

        @pl.when(tm == 0)
        def _():
            ext[frames, 0] = jnp.zeros((size, COLS, CH), BF16)

        @pl.when(tm == bands - 1)
        def _():
            ext[frames, 3] = jnp.zeros((size, COLS, CH), BF16)

        parts = jnp.zeros((cells, 3 * CH), F32)
        for a in range(3):
            parts = parts + dot(ext[frames, a : a + 2].reshape(cells, CH), w_v[a])
        pre = shifted(parts[:, :CH], True) + parts[:, CH : 2 * CH] + shifted(parts[:, 2 * CH :], False)
        sig = jax.nn.sigmoid(pre)
        act = (pre * sig).astype(BF16)
        actx[pl.ds(first + 2, size)] = act.reshape(size, 2 * COLS, CH)
        ag = agrad[frames].reshape(cells, CH).astype(F32)
        pg = ag * sig * (1.0 + pre * (1.0 - sig))
        three = jnp.concatenate([shifted(pg, False), pg, shifted(pg, True)], axis=1).astype(BF16)
        pg3[frames, 1:3] = three.reshape(size, 2, COLS, 3 * CH)
        for a in range(3):
            add_grad(a, dot(ext[frames, a : a + 2].reshape(cells, CH), three, TN))
        cots = jnp.concatenate([cotx[pl.ds(first + k, size)].reshape(cells, CH) for k in range(3)], axis=1)
        add_grad(3, dot(act, cots, TN))

    @pl.loop(0, PAIRS)
    def _(i):
        chunk(i, 2 * i, 2)

    chunk(PAIRS, FRAMES - 1, 1)
    def issue(low, high):
        if low < min(high, PAIRS):
            @pl.loop(low, min(high, PAIRS))
            def _(i):
                for copy in grad_halo(i, 2 * i, 2):
                    copy.start()
        if high > PAIRS:
            for copy in grad_halo(PAIRS, FRAMES - 1, 1):
                copy.start()

    issue(0, 5)

    def mix_unit(i, first, size):
        frames = pl.ds(first, size)
        value = jnp.zeros((size * 2 * COLS, CH), F32)
        for k in range(3):
            value = value + dot(actx[pl.ds(first + 2 - k, size)].reshape(-1, CH), mix_v[k])
        value = value.astype(BF16).astype(F32) + ext[frames, 1:3].reshape(-1, CH).astype(F32)
        out_b[frames] = value.astype(BF16).reshape(size, 2 * COLS, CH)

    def back_unit(i, first, size):
        frames = pl.ds(first, size)
        cells = size * 2 * COLS
        for copy in grad_halo(i, first, size):
            copy.wait_recv()
        for side, row, edge in ((0, 0, 0), (1, 3, bands - 1)):
            value = pgh[side, frames].reshape(size * COLS, CH).astype(F32)
            value = jnp.where(tm == edge, 0.0, value)
            three = jnp.concatenate([shifted(value, False), value, shifted(value, True)], axis=1)
            pg3[frames, row] = three.astype(BF16).reshape(size, COLS, 3 * CH)
        value = cotx[frames].reshape(cells, CH).astype(F32)
        back = jnp.zeros((cells, CH), F32)
        for a in range(3):
            back = back + dot(pg3[frames, 2 - a : 4 - a].reshape(cells, 3 * CH), w_v[a], NT)
        out_g[frames] = (value + back).astype(BF16).reshape(size, 2 * COLS, CH)

    def units(unit, low, high):
        if low < min(high, PAIRS):
            @pl.loop(low, min(high, PAIRS))
            def _(i):
                unit(i, 2 * i, 2)
        if high > PAIRS:
            unit(PAIRS, FRAMES - 1, 1)

    reduce = Reduce(here, grads, total, c_send, c_recv, x_send, x_recv, z_send, z_recv, y_buf, ssem, rsem)
    steps = [reduce.stages(s) for s in range(3)]
    filler = {0: (mix_unit, 0, 3), 1: (mix_unit, 3, 9), 3: (back_unit, 0, 3), 5: (back_unit, 3, 5), 7: (back_unit, 5, 7), 8: (back_unit, 7, 9)}
    for stage in range(10):
        for s in range(3):
            steps[s][stage]()
        if stage == 5:
            issue(5, 9)
        if stage in filler:
            units(*filler[stage])

    reduce.finish()
    over(halo, lambda copy: copy.wait_send())
    over(grad_halo, lambda copy: copy.wait_send())


def tail_kernel(scale, mixed, back, total, block_out, lat_grad, spatial, temporal, wide, sem):
    copies = [pltpu.make_async_copy(mixed, block_out, sem.at[0]), pltpu.make_async_copy(back, lat_grad, sem.at[1])]
    for copy in copies:
        copy.start()
    for a in range(4):
        for t in range(6):
            wide[a, t // 2, :, :, (t % 2) * 128 : (t % 2) * 128 + 128] = total[t, a].astype(F32) * scale
        out = pltpu.make_async_copy(wide.at[a], spatial.at[a] if a < 3 else temporal, sem.at[2 + a])
        out.start()
        copies.append(out)
    for copy in copies:
        copy.wait()


def body(latents, cotangent, spatial_weight, temporal_weight):
    clips, frames, rows, cols, chans = latents.shape
    cells = rows * cols
    any_spec = pl.BlockSpec(memory_space=pl.ANY)
    vmem_spec = pl.BlockSpec(memory_space=pltpu.VMEM)
    half = pltpu.VMEM((frames, cells, chans), BF16)
    results = pl.pallas_call(
        kernel,
        out_shape=(half, half, pltpu.VMEM((6, 4, 8, 32, 128), BF16)),
        in_specs=[any_spec] * 4,
        out_specs=(vmem_spec,) * 3,
        scratch_shapes=[
            pltpu.VMEM((frames, 4, cols, chans), BF16),
            pltpu.VMEM((frames + 2, cells, chans), BF16),
            pltpu.VMEM((frames + 2, cells, chans), BF16),
            pltpu.VMEM((frames, cells, chans), BF16),
            pltpu.VMEM((frames, 4, cols, 3 * chans), BF16),
            pltpu.VMEM((2, frames, cols, chans), BF16),
            pltpu.VMEM((3, chans, 3 * chans), BF16),
            pltpu.VMEM((3, chans, chans), BF16),
            *REDUCE_SCRATCH,
            pltpu.SemaphoreType.DMA((12,)),
            pltpu.SemaphoreType.DMA((2, PAIRS + 1)),
            pltpu.SemaphoreType.DMA((2, PAIRS + 1)),
            pltpu.SemaphoreType.DMA((2, PAIRS + 1)),
            pltpu.SemaphoreType.DMA((2, PAIRS + 1)),
        ],
        compiler_params=pltpu.CompilerParams(
            collective_id=0, has_side_effects=True, vmem_limit_bytes=VMEM_LIMIT
        ),
    )(
        latents.reshape(frames, rows, cols, chans),
        cotangent.reshape(frames, cells, chans),
        spatial_weight,
        temporal_weight,
    )
    scale = (clips * lax.axis_size("dp") * frames * rows * lax.axis_size("tm") * cols) ** (-0.5)
    whole = jax.ShapeDtypeStruct((frames, cells, chans), BF16)
    block_out, lat_grad, spatial, temporal = pl.pallas_call(
        functools.partial(tail_kernel, scale),
        out_shape=(
            whole, whole,
            jax.ShapeDtypeStruct((3, 3, 8, 32, chans), F32), jax.ShapeDtypeStruct((3, 8, 32, chans), F32),
        ),
        in_specs=[vmem_spec] * 3,
        out_specs=(any_spec,) * 4,
        scratch_shapes=[pltpu.VMEM((4, 3, 8, 32, chans), F32), pltpu.SemaphoreType.DMA((6,))],
        compiler_params=pltpu.CompilerParams(vmem_limit_bytes=16 * 1024 * 1024),
    )(*results)
    return (
        block_out.reshape(latents.shape),
        lat_grad.reshape(latents.shape),
        spatial.reshape(3, 3, chans, chans),
        temporal.reshape(3, chans, chans),
    )


def solution(mesh):
    in_specs = (P("dp", None, "tm", None, None), P("dp", None, "tm", None, None), P(), P())
    return jax.shard_map(body, mesh=mesh, in_specs=in_specs, out_specs=in_specs, check_vma=False)
```

```python
import functools

import jax
import jax.numpy as jnp
from jax import lax
from jax.experimental import pallas as pl
from jax.experimental.pallas import tpu as pltpu
from jax.sharding import PartitionSpec as P

F32 = jnp.float32
BF16 = jnp.bfloat16
NX, NY, NZ = 4, 4, 8
FRAMES, COLS, CH = 17, 64, 256
VMEM_LIMIT = 56 * 1024 * 1024
PAIRS = FRAMES // 2
PARTS = FRAMES - PAIRS
EARLY = 6

CORE, XF, XB, XF2, ZS, YS, ZG, XG, CG, SLOTS = 0, 1, 2, 3, 4, 11, 14, 21, 24, 28
SPLIT = 1
ROWS = 32 // SPLIT


def peer(dp, tm):
    return (dp, tm)


def remote(src, dst, send, recv, device):
    return pltpu.make_async_remote_copy(
        src_ref=src, dst_ref=dst, send_sem=send, recv_sem=recv,
        device_id=device, device_id_type=pl.DeviceIdType.MESH,
    )


class Reduce:
    def __init__(self, here, grads, total, c_send, c_recv, x_send, x_recv, z_send, z_recv, y_buf, ssem, rsem):
        self.x, self.core, self.z, self.y = here
        self.grads, self.total = grads, total
        self.c_send, self.c_recv = c_send, c_recv
        self.x_send, self.x_recv = x_send, x_recv
        self.z_send, self.z_recv, self.y_buf = z_send, z_recv, y_buf
        self.ssem, self.rsem = ssem, rsem
        self.copies = {}
        step = 1 - 2 * self.core
        self.fwd = lax.rem(self.x + step + NX, NX)
        self.bwd = lax.rem(self.x - step + NX, NX)
        self.far = lax.rem(self.x + 2, NX)
        self.tm = self.z * NY + self.y

    def at_x(self, x):
        return peer(x * 2 + self.core, self.tm)

    def at_z(self, j):
        z = lax.rem(self.z + j, NZ)
        return z, peer(self.x * 2 + self.core, z * NY + self.y)

    def at_y(self, j):
        return peer(self.x * 2 + self.core, self.z * NY + lax.rem(self.y + j, NY))

    def partner(self):
        return peer(self.x * 2 + 1 - self.core, self.tm)

    def send(self, s, slot, src, dst, device):
        copy = remote(src, dst, self.ssem.at[s, slot], self.rsem.at[s, slot], device)
        copy.start()
        self.copies[s, slot] = copy

    def arrive(self, s, *slots):
        for slot in slots:
            self.copies[s, slot].wait_recv()

    def finish(self):
        for copy in self.copies.values():
            copy.wait_send()

    def stages(self, s):
        part = s // SPLIT
        rows = pl.ds(s % SPLIT * ROWS, ROWS)
        t = self.core * 3 + part
        other = (1 - self.core) * 3 + part
        z = self.z
        x, y = self.x, self.y
        step = 1 - 2 * self.core
        fwd, bwd, far = lax.rem(x + step + NX, NX), lax.rem(x - step + NX, NX), lax.rem(x + 2, NX)

        def at_ring(at):
            return peer(at * 2 + self.core, self.tm)

        def at_cast(j):
            return self.at_y(j)

        hops = (4, 3, 5, 2, 6, 1, 7)

        def local(at):
            return self.grads[t, at, :, rows] + self.c_recv[part, at, :, rows].astype(F32)

        def core_out():
            self.c_send[part, :, :, rows] = self.grads[other, :, :, rows].astype(BF16)
            self.send(s, CORE, self.c_send.at[part, :, :, rows], self.c_recv.at[part, :, :, rows], self.partner())

        def x_send(kind, value, to):
            self.x_send[part, kind, :, rows] = value.astype(BF16)
            self.send(s, XF + kind, self.x_send.at[part, kind, :, rows], self.x_recv.at[part, kind, :, rows], at_ring(to))

        def got(kind):
            return self.x_recv[part, kind, :, rows].astype(F32)

        def first():
            self.arrive(s, CORE)
            x_send(0, local(far), fwd)
            x_send(1, local(bwd), bwd)

        def second():
            self.arrive(s, XF)
            x_send(2, local(fwd) + got(0), fwd)

        def third():
            self.arrive(s, XB, XF2)
            own = local(x) + got(1) + got(2)
            self.grads[t, x, :, rows] = own
            self.z_send[part, 0, :, rows] = own.astype(BF16)
            for j in hops:
                at, device = self.at_z(j)
                self.send(s, ZS + j - 1, self.z_send.at[part, 0, at, rows], self.z_recv.at[part, j - 1, 0, rows], device)

        def fourth():
            self.arrive(s, *range(ZS, ZS + NZ - 1))
            own = self.grads[t, x, z, rows]
            for j in range(NZ - 1):
                own = own + self.z_recv[part, j, 0, rows].astype(F32)
            self.y_buf[part, y, rows] = own.astype(BF16)
            for j in range(1, NY):
                mine = self.y_buf.at[part, y, rows]
                self.send(s, YS + j - 1, mine, mine, at_cast(j))

        def fifth():
            self.arrive(s, *range(YS, YS + NY - 1))
            value = self.y_buf[part, 0, rows].astype(F32)
            for j in range(1, NY):
                value = value + self.y_buf[part, j, rows].astype(F32)
            self.total[t, x, z, rows] = value.astype(BF16)
            block = self.total.at[t, x, z, rows]
            for j in hops:
                self.send(s, ZG + j - 1, block, block, self.at_z(j)[1])

        def sixth():
            self.arrive(s, *range(ZG, ZG + NZ - 1))
            mine = self.total.at[t, x, :, rows]
            self.send(s, XG, mine, mine, at_ring(fwd))
            self.send(s, XG + 1, mine, mine, at_ring(bwd))
            self.send(s, CG, mine, mine, self.partner())

        def seventh():
            self.arrive(s, XG)
            block = self.total.at[t, bwd, :, rows]
            self.send(s, XG + 2, block, block, at_ring(fwd))
            self.send(s, CG + 1, block, block, self.partner())

        def eighth():
            self.arrive(s, XG + 1)
            block = self.total.at[t, fwd, :, rows]
            self.send(s, CG + 2, block, block, self.partner())
            self.arrive(s, XG + 2)
            block = self.total.at[t, far, :, rows]
            self.send(s, CG + 3, block, block, self.partner())

        def ninth():
            self.arrive(s, *range(CG, CG + 4))

        return [core_out, first, second, third, fourth, fifth, sixth, seventh, eighth, ninth]


REDUCE_SCRATCH = [
    pltpu.VMEM((6, 4, 8, 32, 128), F32),
    pltpu.VMEM((3, 4, 8, 32, 128), BF16),
    pltpu.VMEM((3, 4, 8, 32, 128), BF16),
    pltpu.VMEM((3, 3, 8, 32, 128), BF16),
    pltpu.VMEM((3, 3, 8, 32, 128), BF16),
    pltpu.VMEM((3, 4, 8, 32, 128), BF16),
    pltpu.VMEM((3, 7, 4, 32, 128), BF16),
    pltpu.VMEM((3, 4, 32, 128), BF16),
    pltpu.SemaphoreType.DMA((3 * SPLIT, SLOTS)),
    pltpu.SemaphoreType.DMA((3 * SPLIT, SLOTS)),
]


def position():
    dp, tm = lax.axis_index("dp"), lax.axis_index("tm")
    return dp // 2, lax.rem(dp, 2), tm // NY, lax.rem(tm, NY)


def greet(x, core, z, y, extra=()):
    barrier = pltpu.get_barrier_semaphore()
    tm = z * NY + y
    peers = [peer(x * 2 + 1 - core, tm)]
    peers += [peer(lax.rem(x + j, NX) * 2 + core, tm) for j in range(1, NX)]
    peers += [peer(x * 2 + core, z * NY + lax.rem(y + j, NY)) for j in range(1, NY)]
    peers += [peer(x * 2 + core, lax.rem(z + j, NZ) * NY + y) for j in range(1, NZ)]
    peers += list(extra)
    for device in peers:
        pl.semaphore_signal(barrier, inc=1, device_id=device, device_id_type=pl.DeviceIdType.MESH)
    return barrier, len(peers)


NT = (((1,), (1,)), ((), ()))
TN = (((0,), (0,)), ((), ()))


def dot(a, b, dims=(((1,), (0,)), ((), ()))):
    return lax.dot_general(a, b, dims, preferred_element_type=F32)


def shifted(value, up):
    cells = value.shape[0]
    col = lax.rem(lax.broadcasted_iota(jnp.int32, value.shape, 0), COLS)
    if up:
        return jnp.where(col == 0, 0.0, pltpu.roll(value, 1, 0))
    return jnp.where(col == COLS - 1, 0.0, pltpu.roll(value, cells - 1, 0))


def kernel(
    lat, cot, weight, mix, out_b, out_g, total,
    ext, cotx, actx, agrad, pg3, pgh, w_v, w_t, mix_v,
    grads, c_send, c_recv, x_send, x_recv, z_send, z_recv, y_buf, ssem, rsem,
    load_sem, halo_s, halo_r, back_s, back_r,
):
    here = position()
    x, core, z, y = here
    dp, tm = x * 2 + core, z * NY + y
    bands = NZ * NY
    below = peer(dp, lax.rem(tm + 1, bands))
    above = peer(dp, lax.rem(tm + bands - 1, bands))
    barrier, count = greet(x, core, z, y, (above, below))

    loads = [
        pltpu.make_async_copy(cot, cotx.at[pl.ds(0, FRAMES)], load_sem.at[0]),
        pltpu.make_async_copy(mix, mix_v, load_sem.at[1]),
        pltpu.make_async_copy(lat, ext.at[:, pl.ds(1, 2)], load_sem.at[2]),
    ]
    for a in range(3):
        for b in range(3):
            loads.append(pltpu.make_async_copy(weight.at[a, b], w_v.at[a, :, pl.ds(b * CH, CH)], load_sem.at[3 + a * 3 + b]))
    for load in loads:
        load.start()
    cotx[FRAMES:] = jnp.zeros((2, 2 * COLS, CH), BF16)
    actx[:2] = jnp.zeros((2, 2 * COLS, CH), BF16)
    pl.semaphore_wait(barrier, count)

    def halo(i, first, size):
        frames = pl.ds(first, size)
        return (
            remote(lat.at[frames, 1], ext.at[frames, 0], halo_s.at[0, i], halo_r.at[0, i], below),
            remote(lat.at[frames, 0], ext.at[frames, 3], halo_s.at[1, i], halo_r.at[1, i], above),
        )

    def grad_halo(i, first, size):
        frames = pl.ds(first, size)
        return (
            remote(pg3.at[frames, 2, :, pl.ds(CH, CH)], pgh.at[0, frames], back_s.at[0, i], back_r.at[0, i], below),
            remote(pg3.at[frames, 1, :, pl.ds(CH, CH)], pgh.at[1, frames], back_s.at[1, i], back_r.at[1, i], above),
        )

    def over(make, act):
        @pl.loop(0, PAIRS)
        def _(i):
            for copy in make(i, 2 * i, 2):
                act(copy)

        @pl.loop(PAIRS, PARTS)
        def _(i):
            for copy in make(i, i + PAIRS, 1):
                act(copy)

    over(halo, lambda copy: copy.start())

    loads[0].wait()
    loads[1].wait()

    @pl.loop(0, 3)
    def _(i):
        first = jnp.minimum(6 * i, FRAMES - 6)
        value = jnp.zeros((6 * 2 * COLS, CH), F32)
        for k in range(3):
            value = value + dot(cotx[pl.ds(first + k, 6)].reshape(-1, CH), mix_v[k], NT)
        agrad[pl.ds(first, 6)] = value.astype(BF16).reshape(6, 2 * COLS, CH)

    for load in loads[2:]:
        load.wait()

    grads[...] = jnp.zeros_like(grads)

    for a in range(3):
        w_t[a] = w_v[a].T

    def add_grad(index, value):
        for t in range(6):
            grads[t, index] += value[:, t * 128 : (t + 1) * 128].reshape(8, 32, 128)

    def chunk(i, first, size):
        for copy in halo(i, first, size):
            copy.wait_recv()
        frames = pl.ds(first, size)
        cells = size * 2 * COLS
        if size == 1:
            issue(0, EARLY)

        @pl.when(tm == 0)
        def _():
            ext[frames, 0] = jnp.zeros((size, COLS, CH), BF16)

        @pl.when(tm == bands - 1)
        def _():
            ext[frames, 3] = jnp.zeros((size, COLS, CH), BF16)

        parts = jnp.zeros((cells, 3 * CH), F32)
        for a in range(3):
            parts = parts + dot(ext[frames, a : a + 2].reshape(cells, CH), w_v[a])
        pre = shifted(parts[:, :CH], True) + parts[:, CH : 2 * CH] + shifted(parts[:, 2 * CH :], False)
        sig = jax.nn.sigmoid(pre)
        act = (pre * sig).astype(BF16)
        actx[pl.ds(first + 2, size)] = act.reshape(size, 2 * COLS, CH)
        ag = agrad[frames].reshape(cells, CH).astype(F32)
        pg = ag * sig * (1.0 + pre * (1.0 - sig))
        three = jnp.concatenate([shifted(pg, False), pg, shifted(pg, True)], axis=1).astype(BF16)
        pg3[frames, 1:3] = three.reshape(size, 2, COLS, 3 * CH)
        for a in range(3):
            add_grad(a, dot(ext[frames, a : a + 2].reshape(cells, CH), three, TN))
        cots = jnp.concatenate([cotx[pl.ds(first + k, size)].reshape(cells, CH) for k in range(3)], axis=1)
        add_grad(3, dot(act, cots, TN))

    def issue(low, high):
        if low < min(high, PAIRS):
            @pl.loop(low, min(high, PAIRS))
            def _(i):
                for copy in grad_halo(i, 2 * i, 2):
                    copy.start()
        if high > PAIRS:
            @pl.loop(max(low, PAIRS), high)
            def _(i):
                for copy in grad_halo(i, i + PAIRS, 1):
                    copy.start()

    @pl.loop(0, PAIRS)
    def _(i):
        chunk(i, 2 * i, 2)

    @pl.loop(PAIRS, PARTS)
    def _(i):
        chunk(i, i + PAIRS, 1)


    def mix_unit(i, first, size):
        frames = pl.ds(first, size)
        value = jnp.zeros((size * 2 * COLS, CH), F32)
        for k in range(3):
            value = value + dot(actx[pl.ds(first + 2 - k, size)].reshape(-1, CH), mix_v[k])
        value = value.astype(BF16).astype(F32) + ext[frames, 1:3].reshape(-1, CH).astype(F32)
        out_b[frames] = value.astype(BF16).reshape(size, 2 * COLS, CH)

    def back_unit(i, first, size):
        frames = pl.ds(first, size)
        cells = size * 2 * COLS
        for copy in grad_halo(i, first, size):
            copy.wait_recv()
        for side, row, edge in ((0, 0, 0), (1, 3, bands - 1)):
            value = pgh[side, frames].reshape(size * COLS, CH).astype(F32)
            value = jnp.where(tm == edge, 0.0, value)
            three = jnp.concatenate([shifted(value, False), value, shifted(value, True)], axis=1)
            pg3[frames, row] = three.astype(BF16).reshape(size, COLS, 3 * CH)
        value = cotx[frames].reshape(cells, CH).astype(F32)
        back = jnp.zeros((cells, CH), F32)
        for a in range(3):
            back = back + dot(pg3[frames, 2 - a : 4 - a].reshape(cells, 3 * CH), w_t[a])
        out_g[frames] = (value + back).astype(BF16).reshape(size, 2 * COLS, CH)

    def units(unit, low, high):
        if low < min(high, PAIRS):
            @pl.loop(low, min(high, PAIRS))
            def _(i):
                unit(i, 2 * i, 2)
        if high > PAIRS:
            @pl.loop(max(low, PAIRS), high)
            def _(i):
                unit(i, i + PAIRS, 1)

    reduce = Reduce(here, grads, total, c_send, c_recv, x_send, x_recv, z_send, z_recv, y_buf, ssem, rsem)
    steps = [reduce.stages(s) for s in range(3 * SPLIT)]
    events = [(s, k) for k in range(10) for s in range(3 * SPLIT)]
    filler = {0: (mix_unit, 0, 3), 1: (mix_unit, 3, 9), 3: (back_unit, 0, 3), 5: (back_unit, 3, 5), 7: (back_unit, 5, 7), 8: (back_unit, 7, 9)}
    for s, stage in events:
        steps[s][stage]()
        if s == 3 * SPLIT - 1:
            if stage == 5:
                issue(EARLY, PARTS)
            if stage in filler:
                units(*filler[stage])

    reduce.finish()
    over(halo, lambda copy: copy.wait_send())
    over(grad_halo, lambda copy: copy.wait_send())


def tail_kernel(scale, mixed, back, total, block_out, lat_grad, spatial, temporal, wide, sem):
    copies = [pltpu.make_async_copy(mixed, block_out, sem.at[0]), pltpu.make_async_copy(back, lat_grad, sem.at[1])]
    for copy in copies:
        copy.start()
    for a in range(4):
        for t in range(6):
            wide[a, t // 2, :, :, (t % 2) * 128 : (t % 2) * 128 + 128] = total[t, a].astype(F32) * scale
        out = pltpu.make_async_copy(wide.at[a], spatial.at[a] if a < 3 else temporal, sem.at[2 + a])
        out.start()
        copies.append(out)
    for copy in copies:
        copy.wait()


def body(latents, cotangent, spatial_weight, temporal_weight):
    clips, frames, rows, cols, chans = latents.shape
    cells = rows * cols
    any_spec = pl.BlockSpec(memory_space=pl.ANY)
    vmem_spec = pl.BlockSpec(memory_space=pltpu.VMEM)
    half = pltpu.VMEM((frames, cells, chans), BF16)
    results = pl.pallas_call(
        kernel,
        out_shape=(half, half, pltpu.VMEM((6, 4, 8, 32, 128), BF16)),
        in_specs=[any_spec] * 4,
        out_specs=(vmem_spec,) * 3,
        scratch_shapes=[
            pltpu.VMEM((frames, 4, cols, chans), BF16),
            pltpu.VMEM((frames + 2, cells, chans), BF16),
            pltpu.VMEM((frames + 2, cells, chans), BF16),
            pltpu.VMEM((frames, cells, chans), BF16),
            pltpu.VMEM((frames, 4, cols, 3 * chans), BF16),
            pltpu.VMEM((2, frames, cols, chans), BF16),
            pltpu.VMEM((3, chans, 3 * chans), BF16),
            pltpu.VMEM((3, 3 * chans, chans), BF16),
            pltpu.VMEM((3, chans, chans), BF16),
            *REDUCE_SCRATCH,
            pltpu.SemaphoreType.DMA((12,)),
            pltpu.SemaphoreType.DMA((2, PARTS)),
            pltpu.SemaphoreType.DMA((2, PARTS)),
            pltpu.SemaphoreType.DMA((2, PARTS)),
            pltpu.SemaphoreType.DMA((2, PARTS)),
        ],
        compiler_params=pltpu.CompilerParams(
            collective_id=0, has_side_effects=True, vmem_limit_bytes=VMEM_LIMIT
        ),
    )(
        latents.reshape(frames, rows, cols, chans),
        cotangent.reshape(frames, cells, chans),
        spatial_weight,
        temporal_weight,
    )
    scale = (clips * lax.axis_size("dp") * frames * rows * lax.axis_size("tm") * cols) ** (-0.5)
    whole = jax.ShapeDtypeStruct((frames, cells, chans), BF16)
    block_out, lat_grad, spatial, temporal = pl.pallas_call(
        functools.partial(tail_kernel, scale),
        out_shape=(
            whole, whole,
            jax.ShapeDtypeStruct((3, 3, 8, 32, chans), F32), jax.ShapeDtypeStruct((3, 8, 32, chans), F32),
        ),
        in_specs=[vmem_spec] * 3,
        out_specs=(any_spec,) * 4,
        scratch_shapes=[pltpu.VMEM((4, 3, 8, 32, chans), F32), pltpu.SemaphoreType.DMA((6,))],
        compiler_params=pltpu.CompilerParams(vmem_limit_bytes=16 * 1024 * 1024),
    )(*results)
    return (
        block_out.reshape(latents.shape),
        lat_grad.reshape(latents.shape),
        spatial.reshape(3, 3, chans, chans),
        temporal.reshape(3, chans, chans),
    )


def solution(mesh):
    in_specs = (P("dp", None, "tm", None, None), P("dp", None, "tm", None, None), P(), P())
    return jax.shard_map(body, mesh=mesh, in_specs=in_specs, out_specs=in_specs, check_vma=False)
```
